32 devices in a mesh: dp: 8 (over z, core), tensor: 4 (over y, x).
Axes of the slice: x: 2, y: 2, z: 4, core: 2. Of those that a mesh axis runs over, the one named last changes fastest.
Arguments:
- tokens_in: bfloat16 [1024, 8192], P(('dp', 'tensor')), may hold values from -6 to 6
- projector: bfloat16 [8192, 512], P('tensor'), may hold values from -0.0625 to 0.0625
- gate_pre: bfloat16 [1024, 15360], P('dp', 'tensor'), may hold values from -6 to 6
- up_pre: bfloat16 [1024, 15360], P('dp', 'tensor'), may hold values from -6 to 6
- hidden_grad: bfloat16 [1024, 15360], P('dp', 'tensor'), may hold values from -6 to 6
- moment_m: float32 [15360, 1024], P(('tensor', 'dp')), may hold values from -4 to 4
- moment_v: float32 [15360, 1024], P(('tensor', 'dp')), may hold values from 0.05 to 1
Outputs:
- m_next: float32 [15360, 1024], P(('tensor', 'dp'))
- v_next: float32 [15360, 1024], P(('tensor', 'dp'))
- direction: float32 [15360, 1024], P(('tensor', 'dp'))
The draws below stay inside these ranges and needn't reach their ends.
All inputs are finite; a program needn't handle non-finite values.
Results may differ from the reference program's by a relative error of at most 0.00098.
Values may be sent and summed in bfloat16 or wider, within the bound.
A program may use at most 64 MiB of HBM per device.

```python
import math
import jax
import jax.numpy as jnp
from jax import lax

D = 8192
FF = 15360
R = 512
TOK_GRP = 128
TOKENS = 1024


def spiked(drawn, own_key, source, target, shards_of, factor):
    def block_of(axis_at):
        return (jnp.arange(drawn.shape[axis_at]) // (drawn.shape[axis_at] // shards_of)).reshape((-1,) + (1,) * (drawn.ndim - 1 - axis_at))

    first = jax.random.permutation(own_key, shards_of)[block_of(target)]
    far = (block_of(target) + shards_of // 2) % shards_of
    return jnp.where((block_of(source) == first) | (block_of(source) == far), factor * drawn, drawn)


def level_of(rng, extent, pieces, low, high):
    factor_of, own = 1.0, jax.random.fold_in(rng, 6)
    for axis_at, blocks in pieces:
        heights = jnp.exp(jax.random.uniform(jax.random.fold_in(own, axis_at), (blocks,), jnp.float32, low / len(pieces), high / len(pieces)))
        factor_of = factor_of * jnp.repeat(heights, extent[axis_at] // blocks).reshape([-1 if axis == axis_at else 1 for axis in range(len(extent))])
    return factor_of


def centred(rng, shape, deviation, bound, cuts=(), kind=jnp.bfloat16):
    result = deviation * jax.random.normal(rng, shape, jnp.float32)
    if cuts:
        result = result * level_of(rng, shape, cuts, -0.22, 0.18)
    return jnp.clip(result, -bound, bound).astype(kind)


def bell_draw_with(stream_key, extent, scale, most, shards, heavy, dtype=jnp.bfloat16):
    entries = scale * jax.random.normal(stream_key, extent, jnp.float32)
    if shards:
        entries = entries * level_of(stream_key, extent, shards, -0.22, 0.18)
    return jnp.clip(spiked(entries, jax.random.fold_in(stream_key, 3), *heavy), -most, most).astype(dtype)


def setup_inputs(seed: int = 0) -> dict:
    splits = jax.random.split(jax.random.key(seed), 8)
    return {
        "tokens_in": centred(splits[0], (TOKENS, D), 1.0, 6.0, ((0, 32),)),
        "projector": centred(splits[1], (D, R), D ** -0.5, 0.0625, ((0, 4),)),
        "gate_pre": centred(splits[2], (TOKENS, FF), 1.0, 6.0, ((0, 8), (1, 4))),
        "up_pre": centred(splits[3], (TOKENS, FF), 1.0, 6.0, ((0, 8), (1, 4))),
        "hidden_grad": bell_draw_with(splits[4], (TOKENS, FF), 1.0, 6.0, ((0, 8), (1, 4)), (0, 1, 8, 2.0)),
        "moment_m": centred(splits[5], (FF, 2 * R), 0.5, 4.0, ((0, 32),), jnp.float32),
        "moment_v": jnp.clip(jnp.exp(math.log(1.0) - 2.9957323 * jax.random.uniform(splits[6], (FF, 2 * R), jnp.float32) ** level_of(splits[6], (FF, 2 * R), ((0, 32),), -0.2, 0.2)), 0.05, 1.0),
    }


def group_terms(gate_blk, up_blk, hgrad_blk, xp_blk):
    gate = gate_blk.astype(jnp.float32)
    upval = up_blk.astype(jnp.float32)
    hgrad = hgrad_blk.astype(jnp.float32)
    sig = jax.nn.sigmoid(gate)
    grad_gate = (hgrad * upval * sig * (1.0 + gate * (1.0 - sig))).astype(jnp.bfloat16)
    grad_up = (hgrad * gate * sig).astype(jnp.bfloat16)
    first = jnp.dot(grad_gate.T, xp_blk, preferred_element_type=jnp.float32)
    second = jnp.dot(grad_up.T, xp_blk, preferred_element_type=jnp.float32)
    return jnp.concatenate([first, second], axis=1)

def reference(tokens_in, projector, gate_pre, up_pre, hidden_grad, moment_m, moment_v):
    groups = gate_pre.shape[0] // TOK_GRP
    xp = jnp.dot(tokens_in, projector, preferred_element_type=jnp.float32).astype(jnp.bfloat16)
    width = gate_pre.shape[1]
    stacked = (gate_pre.reshape(groups, TOK_GRP, width), up_pre.reshape(groups, TOK_GRP, width), hidden_grad.reshape(groups, TOK_GRP, width), xp.reshape(groups, TOK_GRP, xp.shape[1]))

    def accumulate(total, blocks):
        return (total + group_terms(blocks[0], blocks[1], blocks[2], blocks[3]), None)
    start = jnp.zeros((width, 2 * xp.shape[1]), jnp.float32)
    total, unused = lax.scan(accumulate, start, stacked)
    proj = total * float(TOKENS) ** (-0.5)
    m_next = 0.9 * moment_m + 0.1 * proj
    v_next = 0.95 * moment_v + 0.05 * proj * proj
    direction = m_next / (jnp.sqrt(v_next) + 1e-08)
    return (m_next, v_next, direction)
```

```python
import jax
import jax.numpy as jnp
from jax import lax
from jax.sharding import PartitionSpec as P


def finish(summed, total_tokens, moment_m, moment_v):
    proj = summed * float(total_tokens) ** (-0.5)
    m_next = 0.9 * moment_m + 0.1 * proj
    v_next = 0.95 * moment_v + 0.05 * proj * proj
    direction = m_next / (jnp.sqrt(v_next) + 1e-08)
    return (m_next, v_next, direction)


def local(tokens_in, projector, gate_pre, up_pre, hidden_grad, moment_m, moment_v):
    gate = gate_pre.astype(jnp.float32)
    hgrad = hidden_grad.astype(jnp.float32)
    sig = jax.nn.sigmoid(gate)
    upval = up_pre.astype(jnp.float32)
    grad_gate = (hgrad * upval * sig * (1.0 + gate * (1.0 - sig))).astype(jnp.bfloat16)
    grad_up = (hgrad * gate * sig).astype(jnp.bfloat16)
    grads = jnp.stack([grad_gate, grad_up])
    grads = lax.all_to_all(grads, "dp", split_axis=2, concat_axis=1, tiled=True)
    columns = lax.all_to_all(tokens_in, "tensor", split_axis=1, concat_axis=0, tiled=True)
    partial_xp = jnp.dot(columns, projector, preferred_element_type=jnp.float32)
    own_rows = lax.psum_scatter(partial_xp, "tensor", scatter_dimension=0, tiled=True).astype(
        jnp.bfloat16
    )
    xp = lax.all_gather(own_rows, ("dp", "tensor"), axis=0, tiled=True)
    contract = (((0,), (0,)), ((), ()))
    halves = [
        lax.dot_general(grads[k], xp, contract, preferred_element_type=jnp.float32) for k in (0, 1)
    ]
    summed = jnp.concatenate(halves, axis=1)
    return finish(summed, xp.shape[0], moment_m, moment_v)


def solution(mesh):
    return jax.shard_map(
        local,
        mesh=mesh,
        in_specs=(
            P(("dp", "tensor"), None),
            P("tensor", None),
            P("dp", "tensor"),
            P("dp", "tensor"),
            P("dp", "tensor"),
            P(("tensor", "dp"), None),
            P(("tensor", "dp"), None),
        ),
        out_specs=(P(("tensor", "dp"), None), P(("tensor", "dp"), None), P(("tensor", "dp"), None)),
        check_vma=False,
    )
```

```python
import functools

import jax
import jax.numpy as jnp
from jax import lax
from jax.experimental import pallas as pl
from jax.experimental.pallas import tpu as pltpu
from jax.sharding import PartitionSpec as P


MESH = pl.DeviceIdType.MESH


def exchange_kernel(
    ndp, nt, tok_ref, prj_ref, gate_ref, up_ref, hg_ref, out_ref,
    g_v, u_v, h_v, prj_v, cols, part, rs_buf, xp_all, grads, recv,
    load_sem, tok_send, tok_recv, rs_send, rs_recv,
    xz_send, xt_send, xc_send, xp_recv, xc_recv, g_send, g_recv,
):
    d = lax.axis_index("dp")
    t = lax.axis_index("tensor")
    nz = ndp // 2
    z, c = d // 2, d % 2
    sub = tok_ref.shape[0]
    grp = sub * nt
    dcol = tok_ref.shape[1] // nt
    rows = recv.shape[2]
    rank = prj_ref.shape[1]
    half = ndp // 2
    half_tiles = half * rows // 128

    barrier = pltpu.get_barrier_semaphore()
    for k in range(1, ndp):
        pl.semaphore_signal(barrier, inc=1, device_id=((d + k) % ndp, t), device_id_type=MESH)
    for k in range(1, nt):
        pl.semaphore_signal(barrier, inc=1, device_id=(d, (t + k) % nt), device_id_type=MESH)

    loads = [
        pltpu.make_async_copy(src, dst, load_sem.at[i])
        for i, (src, dst) in enumerate(
            ((gate_ref, g_v), (up_ref, u_v), (hg_ref, h_v), (prj_ref, prj_v))
        )
    ]
    own_tok = pltpu.make_async_copy(
        tok_ref.at[:, pl.ds(pl.multiple_of(t * dcol, 128), dcol)],
        cols.at[pl.ds(pl.multiple_of(t * sub, 16), sub), :],
        load_sem.at[4],
    )
    for load in loads:
        load.start()
    own_tok.start()
    pl.semaphore_wait(barrier, ndp + nt - 2)

    def tok_copy(dest, src):
        return pltpu.make_async_remote_copy(
            src_ref=tok_ref.at[:, pl.ds(pl.multiple_of(dest * dcol, 128), dcol)],
            dst_ref=cols.at[pl.ds(pl.multiple_of(src * sub, 16), sub), :],
            send_sem=tok_send.at[dest],
            recv_sem=tok_recv.at[src],
            device_id=(d, dest),
            device_id_type=MESH,
        )

    for k in range(1, nt):
        tok_copy((t + k) % nt, t).start()

    for load in loads[:3]:
        load.wait()

    def tile(i, carry):
        at = pl.ds(pl.multiple_of(i * 128, 128), 128)
        gate = g_v[:, at].astype(jnp.float32)
        upval = u_v[:, at].astype(jnp.float32)
        hgrad = h_v[:, at].astype(jnp.float32)
        sig = jax.nn.sigmoid(gate)
        grad_gate = hgrad * upval * sig * (1.0 + gate * (1.0 - sig))
        grad_up = hgrad * gate * sig
        grads[0, at, :] = grad_gate.astype(jnp.bfloat16).T
        grads[1, at, :] = grad_up.astype(jnp.bfloat16).T
        return carry

    def block_of(dest):
        return grads.at[:, pl.ds(pl.multiple_of(dest * rows, 16), rows), :]

    def grad_copy(dest, src):
        return pltpu.make_async_remote_copy(
            src_ref=block_of(dest),
            dst_ref=recv.at[src],
            send_sem=g_send.at[dest],
            recv_sem=g_recv.at[src],
            device_id=(dest, t),
            device_id_type=MESH,
        )

    own_grad = pltpu.make_async_copy(block_of(d), recv.at[d], load_sem.at[5])

    own_half = d // half
    inner = (z * (nz - 1 - z) + nz * nz - 1) // (nz * nz)
    first = own_half * (1 - inner) + (1 - own_half) * inner

    def send_block(dest):
        @pl.when(dest != d)
        def _():
            grad_copy(dest, d).start()

        @pl.when(dest == d)
        def _():
            own_grad.start()

    def tiles_of(which, start, stop):
        lax.fori_loop(which * half_tiles + start, which * half_tiles + stop, tile, 0)

    done = 0
    for j in range(half):
        need = -(-((j + 1) * rows) // 128)
        tiles_of(first, done, need)
        done = need
        send_block(first * half + j)
    tiles_of(1 - first, 0, half_tiles)

    loads[3].wait()
    own_tok.wait()
    for k in range(1, nt):
        tok_copy(t, (t + k) % nt).wait_recv()
    part[...] = jnp.dot(cols[...], prj_v[...], preferred_element_type=jnp.float32)

    def rs_copy(dest, src):
        return pltpu.make_async_remote_copy(
            src_ref=part.at[pl.ds(pl.multiple_of(dest * sub, 16), sub), :],
            dst_ref=rs_buf.at[src],
            send_sem=rs_send.at[dest],
            recv_sem=rs_recv.at[src],
            device_id=(d, dest),
            device_id_type=MESH,
        )

    for k in range(1, nt):
        rs_copy((t + k) % nt, t).start()
    rs_buf[t] = part[pl.ds(pl.multiple_of(t * sub, 16), sub), :]
    for k in range(1, nt):
        rs_copy(t, (t + k) % nt).wait_recv()
    total = rs_buf[0]
    for k in range(1, nt):
        total = total + rs_buf[k]

    def piece(dd, tt):
        return xp_all.at[pl.ds(pl.multiple_of(dd * grp + tt * sub, 16), sub), :]

    xp_all[pl.ds(pl.multiple_of(d * grp + t * sub, 16), sub), :] = total.astype(jnp.bfloat16)

    def piece_copy(dd, tt, send_sem, dest):
        return pltpu.make_async_remote_copy(
            src_ref=piece(dd, tt),
            dst_ref=piece(dd, tt),
            send_sem=send_sem,
            recv_sem=xp_recv.at[dd * nt + tt],
            device_id=dest,
            device_id_type=MESH,
        )

    for k in range(1, nz):
        zz = (z + k) % nz
        piece_copy(d, t, xz_send.at[zz], (zz * 2 + c, t)).start()

    for j in range(half):
        send_block((1 - first) * half + j)

    if nz == 4:
        order = [z, z + 1 - 2 * (z % 2), 2 - z // 2, 3 - 3 * (z // 2)]
    else:
        order = [(z + k) % nz for k in range(nz)]

    for k, zz in enumerate(order):
        dd = zz * 2 + c
        if k:
            piece_copy(dd, t, xz_send.at[zz], (dd, t)).wait_recv()
        for kt in range(1, nt):
            tt = (t + kt) % nt
            piece_copy(dd, t, xt_send.at[zz * nt + tt], (d, tt)).start()

    partner = d + 1 - 2 * c

    def core_copy(zz, parity):
        group = xp_all.at[pl.ds(pl.multiple_of((zz * 2 + parity) * grp, 128), grp), :]
        return pltpu.make_async_remote_copy(
            src_ref=group,
            dst_ref=group,
            send_sem=xc_send.at[zz],
            recv_sem=xc_recv.at[zz],
            device_id=(partner, t),
            device_id_type=MESH,
        )

    for zz in order:
        for kt in range(1, nt):
            tt = (t + kt) % nt
            piece_copy(zz * 2 + c, tt, xt_send.at[zz * nt + tt], (d, tt)).wait_recv()
        core_copy(zz, c).start()

    for k, zz in enumerate(order):
        core_copy(zz, 1 - c).wait_recv()
        if k == 0:
            own_grad.wait()
            grad_copy(d, partner).wait_recv()
        else:
            grad_copy(d, zz * 2).wait_recv()
            grad_copy(d, zz * 2 + 1).wait_recv()
        xp = xp_all[pl.ds(pl.multiple_of(zz * 2 * grp, 128), 2 * grp), :]
        for part_of in (0, 1):
            lhs = jnp.concatenate([recv[zz * 2, part_of], recv[zz * 2 + 1, part_of]], axis=1)
            term = jnp.dot(lhs, xp, preferred_element_type=jnp.float32)
            at = slice(part_of * rank, (part_of + 1) * rank)
            if k == 0:
                out_ref[:, at] = term
            else:
                out_ref[:, at] += term

    for k in range(1, nt):
        dest = (t + k) % nt
        tok_copy(dest, t).wait_send()
        rs_copy(dest, t).wait_send()
        for zz in range(nz):
            piece_copy(zz * 2 + c, t, xt_send.at[zz * nt + dest], (d, dest)).wait_send()
    for k in range(1, nz):
        zz = (z + k) % nz
        piece_copy(d, t, xz_send.at[zz], (zz * 2 + c, t)).wait_send()
    for zz in range(nz):
        core_copy(zz, c).wait_send()
    for k in range(1, ndp):
        grad_copy((d + k) % ndp, d).wait_send()


def exchange(ndp, nt, tokens_in, projector, gate_pre, up_pre, hidden_grad):
    sub, width = tokens_in.shape
    depth, rank = projector.shape
    grp, cols = gate_pre.shape
    rows = cols // ndp
    dma = pltpu.SemaphoreType.DMA
    bf, f32 = jnp.bfloat16, jnp.float32
    nz = ndp // 2
    flops = 2 * grp * depth * rank + 4 * rows * grp * ndp * rank
    return pl.pallas_call(
        functools.partial(exchange_kernel, ndp, nt),
        out_shape=jax.ShapeDtypeStruct((rows, 2 * rank), f32),
        in_specs=[pl.BlockSpec(memory_space=pl.ANY)] * 5,
        out_specs=pl.BlockSpec(memory_space=pltpu.VMEM),
        scratch_shapes=[
            pltpu.VMEM((grp, cols), bf),
            pltpu.VMEM((grp, cols), bf),
            pltpu.VMEM((grp, cols), bf),
            pltpu.VMEM((depth, rank), bf),
            pltpu.VMEM((grp, depth), bf),
            pltpu.VMEM((grp, rank), f32),
            pltpu.VMEM((nt, sub, rank), f32),
            pltpu.VMEM((grp * ndp, rank), bf),
            pltpu.VMEM((2, cols, grp), bf),
            pltpu.VMEM((ndp, 2, rows, grp), bf),
            dma((6,)),
            dma((nt,)),
            dma((nt,)),
            dma((nt,)),
            dma((nt,)),
            dma((nz,)),
            dma((nz * nt,)),
            dma((nz,)),
            dma((ndp * nt,)),
            dma((nz,)),
            dma((ndp,)),
            dma((ndp,)),
        ],
        compiler_params=pltpu.CompilerParams(
            collective_id=0, has_side_effects=True, vmem_limit_bytes=32 * 1024 * 1024
        ),
        cost_estimate=pl.CostEstimate(
            flops=flops, bytes_accessed=8 * grp * cols, transcendentals=grp * cols
        ),
    )(tokens_in, projector, gate_pre, up_pre, hidden_grad)


def fits(ndp, nt, tokens_in, projector, gate_pre):
    sub, width = tokens_in.shape
    grp, cols = gate_pre.shape
    return (
        ndp % 2 == 0
        and ndp >= 4
        and nt >= 2
        and grp == 128
        and sub * nt == grp
        and sub % 16 == 0
        and cols % ndp == 0
        and (cols // ndp) % 16 == 0
        and cols % 256 == 0
        and width % (128 * nt) == 0
        and projector.shape[0] == width // nt
        and projector.shape[1] % 128 == 0
        and cols <= 8192
        and projector.size <= 2**21
        and grp * ndp <= 4096
    )


def finish(summed, total_tokens, moment_m, moment_v):
    proj = summed * float(total_tokens) ** (-0.5)
    m_next = 0.9 * moment_m + 0.1 * proj
    v_next = 0.95 * moment_v + 0.05 * proj * proj
    direction = m_next / (jnp.sqrt(v_next) + 1e-08)
    return (m_next, v_next, direction)


def local(tokens_in, projector, gate_pre, up_pre, hidden_grad, moment_m, moment_v):
    ndp, nt = lax.axis_size("dp"), lax.axis_size("tensor")
    if fits(ndp, nt, tokens_in, projector, gate_pre):
        summed = exchange(ndp, nt, tokens_in, projector, gate_pre, up_pre, hidden_grad)
        return finish(summed, gate_pre.shape[0] * ndp, moment_m, moment_v)
    gate = gate_pre.astype(jnp.float32)
    hgrad = hidden_grad.astype(jnp.float32)
    sig = jax.nn.sigmoid(gate)
    upval = up_pre.astype(jnp.float32)
    grad_gate = (hgrad * upval * sig * (1.0 + gate * (1.0 - sig))).astype(jnp.bfloat16)
    grad_up = (hgrad * gate * sig).astype(jnp.bfloat16)
    grads = jnp.stack([grad_gate, grad_up])
    grads = lax.all_to_all(grads, "dp", split_axis=2, concat_axis=1, tiled=True)
    columns = lax.all_to_all(tokens_in, "tensor", split_axis=1, concat_axis=0, tiled=True)
    partial_xp = jnp.dot(columns, projector, preferred_element_type=jnp.float32)
    own_rows = lax.psum_scatter(partial_xp, "tensor", scatter_dimension=0, tiled=True).astype(
        jnp.bfloat16
    )
    xp = lax.all_gather(own_rows, ("dp", "tensor"), axis=0, tiled=True)
    contract = (((0,), (0,)), ((), ()))
    halves = [
        lax.dot_general(grads[k], xp, contract, preferred_element_type=jnp.float32) for k in (0, 1)
    ]
    summed = jnp.concatenate(halves, axis=1)
    return finish(summed, xp.shape[0], moment_m, moment_v)


def solution(mesh):
    return jax.shard_map(
        local,
        mesh=mesh,
        in_specs=(
            P(("dp", "tensor"), None),
            P("tensor", None),
            P("dp", "tensor"),
            P("dp", "tensor"),
            P("dp", "tensor"),
            P(("tensor", "dp"), None),
            P(("tensor", "dp"), None),
        ),
        out_specs=(P(("tensor", "dp"), None), P(("tensor", "dp"), None), P(("tensor", "dp"), None)),
        check_vma=False,
    )
```

```python
import functools

import jax
import jax.numpy as jnp
from jax import lax
from jax.experimental import pallas as pl
from jax.experimental.pallas import tpu as pltpu
from jax.sharding import PartitionSpec as P


MESH = pl.DeviceIdType.MESH


def exchange_kernel(
    ndp, nt, tok_ref, prj_ref, gate_ref, up_ref, hg_ref, out_ref,
    g_v, u_v, h_v, prj_v, cols, part, rs_buf, xp_all, grads, recv,
    load_sem, tok_send, tok_recv, rs_send, rs_recv,
    xz_send, xt_send, xc_send, xp_recv, xc_recv, g_send, g_recv,
):
    d = lax.axis_index("dp")
    t = lax.axis_index("tensor")
    nz = ndp // 2
    z, c = d // 2, d % 2
    sub = tok_ref.shape[0]
    grp = sub * nt
    dcol = tok_ref.shape[1] // nt
    rows = recv.shape[2]
    rank = prj_ref.shape[1]
    half = ndp // 2
    half_tiles = half * rows // 128

    own_half = d // half
    inner = (z * (nz - 1 - z) + nz * nz - 1) // (nz * nz)
    first = own_half * (1 - inner) + (1 - own_half) * inner

    head = -(-rows // 128)
    spans = (
        (first * half_tiles, head),
        (first * half_tiles + head, half_tiles - head),
        ((1 - first) * half_tiles, half_tiles),
    )
    loads = []
    for i, (start, count) in enumerate(spans):
        at = pl.ds(pl.multiple_of(start * 128, 128), count * 128)
        for k, (src, dst) in enumerate(((gate_ref, g_v), (up_ref, u_v), (hg_ref, h_v))):
            loads.append(
                pltpu.make_async_copy(src.at[:, at], dst.at[:, at], load_sem.at[3 * i + k])
            )
    load_prj = pltpu.make_async_copy(prj_ref, prj_v, load_sem.at[9])
    own_tok = pltpu.make_async_copy(
        tok_ref.at[:, pl.ds(pl.multiple_of(t * dcol, 128), dcol)],
        cols.at[pl.ds(pl.multiple_of(t * sub, 16), sub), :],
        load_sem.at[10],
    )
    for load in loads[:3]:
        load.start()

    barrier = pltpu.get_barrier_semaphore()
    for k in range(1, ndp):
        pl.semaphore_signal(barrier, inc=1, device_id=((d + k) % ndp, t), device_id_type=MESH)
    for k in range(1, nt):
        pl.semaphore_signal(barrier, inc=1, device_id=(d, (t + k) % nt), device_id_type=MESH)

    for load in loads[3:]:
        load.start()
    load_prj.start()
    own_tok.start()

    def tok_copy(dest, src):
        return pltpu.make_async_remote_copy(
            src_ref=tok_ref.at[:, pl.ds(pl.multiple_of(dest * dcol, 128), dcol)],
            dst_ref=cols.at[pl.ds(pl.multiple_of(src * sub, 16), sub), :],
            send_sem=tok_send.at[dest],
            recv_sem=tok_recv.at[src],
            device_id=(d, dest),
            device_id_type=MESH,
        )

    def tile(i, carry):
        at = pl.ds(pl.multiple_of(i * 128, 128), 128)
        gate = g_v[:, at].astype(jnp.float32)
        upval = u_v[:, at].astype(jnp.float32)
        hgrad = h_v[:, at].astype(jnp.float32)
        sig = jax.nn.sigmoid(gate)
        grad_gate = hgrad * upval * sig * (1.0 + gate * (1.0 - sig))
        grad_up = hgrad * gate * sig
        grads[0, at, :] = grad_gate.astype(jnp.bfloat16).T
        grads[1, at, :] = grad_up.astype(jnp.bfloat16).T
        return carry

    def block_of(dest):
        return grads.at[:, pl.ds(pl.multiple_of(dest * rows, 16), rows), :]

    def grad_copy(dest, src):
        return pltpu.make_async_remote_copy(
            src_ref=block_of(dest),
            dst_ref=recv.at[src],
            send_sem=g_send.at[dest],
            recv_sem=g_recv.at[src],
            device_id=(dest, t),
            device_id_type=MESH,
        )

    own_grad = pltpu.make_async_copy(block_of(d), recv.at[d], load_sem.at[11])

    def send_block(dest):
        @pl.when(dest != d)
        def _():
            grad_copy(dest, d).start()

        @pl.when(dest == d)
        def _():
            own_grad.start()

    def tiles_of(which, start, stop):
        lax.fori_loop(which * half_tiles + start, which * half_tiles + stop, tile, 0)

    for load in loads[:3]:
        load.wait()
    tiles_of(first, 0, head)
    pl.semaphore_wait(barrier, ndp + nt - 2)
    send_block(first * half)
    for k in range(1, nt):
        tok_copy((t + k) % nt, t).start()

    for load in loads[3:6]:
        load.wait()
    done = head
    for j in range(1, half):
        need = -(-((j + 1) * rows) // 128)
        tiles_of(first, done, need)
        done = need
        send_block(first * half + j)
    for load in loads[6:]:
        load.wait()
    tiles_of(1 - first, 0, half_tiles)

    load_prj.wait()
    own_tok.wait()
    for k in range(1, nt):
        tok_copy(t, (t + k) % nt).wait_recv()
    part[...] = jnp.dot(cols[...], prj_v[...], preferred_element_type=jnp.float32)

    def rs_copy(dest, src):
        return pltpu.make_async_remote_copy(
            src_ref=part.at[pl.ds(pl.multiple_of(dest * sub, 16), sub), :],
            dst_ref=rs_buf.at[src],
            send_sem=rs_send.at[dest],
            recv_sem=rs_recv.at[src],
            device_id=(d, dest),
            device_id_type=MESH,
        )

    for k in range(1, nt):
        rs_copy((t + k) % nt, t).start()
    rs_buf[t] = part[pl.ds(pl.multiple_of(t * sub, 16), sub), :]
    for k in range(1, nt):
        rs_copy(t, (t + k) % nt).wait_recv()
    total = rs_buf[0]
    for k in range(1, nt):
        total = total + rs_buf[k]

    def piece(dd, tt):
        return xp_all.at[pl.ds(pl.multiple_of(dd * grp + tt * sub, 16), sub), :]

    xp_all[pl.ds(pl.multiple_of(d * grp + t * sub, 16), sub), :] = total.astype(jnp.bfloat16)

    def piece_copy(dd, tt, send_sem, dest):
        return pltpu.make_async_remote_copy(
            src_ref=piece(dd, tt),
            dst_ref=piece(dd, tt),
            send_sem=send_sem,
            recv_sem=xp_recv.at[dd * nt + tt],
            device_id=dest,
            device_id_type=MESH,
        )

    for k in range(1, nz):
        zz = (z + k) % nz
        piece_copy(d, t, xz_send.at[zz], (zz * 2 + c, t)).start()

    for j in range(half):
        send_block((1 - first) * half + j)

    if nz == 4:
        order = [z, z + 1 - 2 * (z % 2), 2 - z // 2, 3 - 3 * (z // 2)]
    else:
        order = [(z + k) % nz for k in range(nz)]

    for k, zz in enumerate(order):
        dd = zz * 2 + c
        if k:
            piece_copy(dd, t, xz_send.at[zz], (dd, t)).wait_recv()
        for kt in range(1, nt):
            tt = (t + kt) % nt
            piece_copy(dd, t, xt_send.at[zz * nt + tt], (d, tt)).start()

    partner = d + 1 - 2 * c

    def core_copy(zz, parity):
        group = xp_all.at[pl.ds(pl.multiple_of((zz * 2 + parity) * grp, 128), grp), :]
        return pltpu.make_async_remote_copy(
            src_ref=group,
            dst_ref=group,
            send_sem=xc_send.at[zz],
            recv_sem=xc_recv.at[zz],
            device_id=(partner, t),
            device_id_type=MESH,
        )

    for zz in order:
        for kt in range(1, nt):
            tt = (t + kt) % nt
            piece_copy(zz * 2 + c, tt, xt_send.at[zz * nt + tt], (d, tt)).wait_recv()
        core_copy(zz, c).start()

    for k, zz in enumerate(order):
        core_copy(zz, 1 - c).wait_recv()
        if k == 0:
            own_grad.wait()
            grad_copy(d, partner).wait_recv()
        else:
            grad_copy(d, zz * 2).wait_recv()
            grad_copy(d, zz * 2 + 1).wait_recv()
        xp = xp_all[pl.ds(pl.multiple_of(zz * 2 * grp, 128), 2 * grp), :]
        for part_of in (0, 1):
            lhs = jnp.concatenate([recv[zz * 2, part_of], recv[zz * 2 + 1, part_of]], axis=1)
            term = jnp.dot(lhs, xp, preferred_element_type=jnp.float32)
            at = slice(part_of * rank, (part_of + 1) * rank)
            if k == 0:
                out_ref[:, at] = term
            else:
                out_ref[:, at] += term

    for k in range(1, nt):
        dest = (t + k) % nt
        tok_copy(dest, t).wait_send()
        rs_copy(dest, t).wait_send()
        for zz in range(nz):
            piece_copy(zz * 2 + c, t, xt_send.at[zz * nt + dest], (d, dest)).wait_send()
    for k in range(1, nz):
        zz = (z + k) % nz
        piece_copy(d, t, xz_send.at[zz], (zz * 2 + c, t)).wait_send()
    for zz in range(nz):
        core_copy(zz, c).wait_send()
    for k in range(1, ndp):
        grad_copy((d + k) % ndp, d).wait_send()


def exchange(ndp, nt, tokens_in, projector, gate_pre, up_pre, hidden_grad):
    sub, width = tokens_in.shape
    depth, rank = projector.shape
    grp, cols = gate_pre.shape
    rows = cols // ndp
    dma = pltpu.SemaphoreType.DMA
    bf, f32 = jnp.bfloat16, jnp.float32
    nz = ndp // 2
    operands = (tokens_in, projector, gate_pre, up_pre, hidden_grad)
    flops = 2 * grp * depth * rank + 4 * rows * grp * ndp * rank
    return pl.pallas_call(
        functools.partial(exchange_kernel, ndp, nt),
        out_shape=jax.ShapeDtypeStruct((rows, 2 * rank), f32),
        in_specs=[pl.BlockSpec(memory_space=pltpu.HBM)] * 5,
        out_specs=pl.BlockSpec(memory_space=pltpu.VMEM),
        scratch_shapes=[
            pltpu.VMEM((grp, cols), bf),
            pltpu.VMEM((grp, cols), bf),
            pltpu.VMEM((grp, cols), bf),
            pltpu.VMEM((depth, rank), bf),
            pltpu.VMEM((grp, depth), bf),
            pltpu.VMEM((grp, rank), f32),
            pltpu.VMEM((nt, sub, rank), f32),
            pltpu.VMEM((grp * ndp, rank), bf),
            pltpu.VMEM((2, cols, grp), bf),
            pltpu.VMEM((ndp, 2, rows, grp), bf),
            dma((12,)),
            dma((nt,)),
            dma((nt,)),
            dma((nt,)),
            dma((nt,)),
            dma((nz,)),
            dma((nz * nt,)),
            dma((nz,)),
            dma((ndp * nt,)),
            dma((nz,)),
            dma((ndp,)),
            dma((ndp,)),
        ],
        compiler_params=pltpu.CompilerParams(
            collective_id=0, has_side_effects=True, vmem_limit_bytes=32 * 1024 * 1024
        ),
        cost_estimate=pl.CostEstimate(
            flops=flops, bytes_accessed=8 * grp * cols, transcendentals=grp * cols
        ),
    )(*[pltpu.with_memory_space_constraint(x, pltpu.HBM) for x in operands])


def fits(ndp, nt, tokens_in, projector, gate_pre):
    sub, width = tokens_in.shape
    grp, cols = gate_pre.shape
    return (
        ndp % 2 == 0
        and ndp >= 4
        and nt >= 2
        and grp == 128
        and sub * nt == grp
        and sub % 16 == 0
        and cols % ndp == 0
        and (cols // ndp) % 16 == 0
        and cols % 256 == 0
        and width % (128 * nt) == 0
        and projector.shape[0] == width // nt
        and projector.shape[1] % 128 == 0
        and cols <= 8192
        and projector.size <= 2**21
        and grp * ndp <= 4096
    )


def finish(summed, total_tokens, moment_m, moment_v):
    proj = summed * float(total_tokens) ** (-0.5)
    m_next = 0.9 * moment_m + 0.1 * proj
    v_next = 0.95 * moment_v + 0.05 * proj * proj
    direction = m_next / (jnp.sqrt(v_next) + 1e-08)
    return (m_next, v_next, direction)


def local(tokens_in, projector, gate_pre, up_pre, hidden_grad, moment_m, moment_v):
    ndp, nt = lax.axis_size("dp"), lax.axis_size("tensor")
    if fits(ndp, nt, tokens_in, projector, gate_pre):
        summed = exchange(ndp, nt, tokens_in, projector, gate_pre, up_pre, hidden_grad)
        return finish(summed, gate_pre.shape[0] * ndp, moment_m, moment_v)
    gate = gate_pre.astype(jnp.float32)
    hgrad = hidden_grad.astype(jnp.float32)
    sig = jax.nn.sigmoid(gate)
    upval = up_pre.astype(jnp.float32)
    grad_gate = (hgrad * upval * sig * (1.0 + gate * (1.0 - sig))).astype(jnp.bfloat16)
    grad_up = (hgrad * gate * sig).astype(jnp.bfloat16)
    grads = jnp.stack([grad_gate, grad_up])
    grads = lax.all_to_all(grads, "dp", split_axis=2, concat_axis=1, tiled=True)
    columns = lax.all_to_all(tokens_in, "tensor", split_axis=1, concat_axis=0, tiled=True)
    partial_xp = jnp.dot(columns, projector, preferred_element_type=jnp.float32)
    own_rows = lax.psum_scatter(partial_xp, "tensor", scatter_dimension=0, tiled=True).astype(
        jnp.bfloat16
    )
    xp = lax.all_gather(own_rows, ("dp", "tensor"), axis=0, tiled=True)
    contract = (((0,), (0,)), ((), ()))
    halves = [
        lax.dot_general(grads[k], xp, contract, preferred_element_type=jnp.float32) for k in (0, 1)
    ]
    summed = jnp.concatenate(halves, axis=1)
    return finish(summed, xp.shape[0], moment_m, moment_v)


def solution(mesh):
    return jax.shard_map(
        local,
        mesh=mesh,
        in_specs=(
            P(("dp", "tensor"), None),
            P("tensor", None),
            P("dp", "tensor"),
            P("dp", "tensor"),
            P("dp", "tensor"),
            P(("tensor", "dp"), None),
            P(("tensor", "dp"), None),
        ),
        out_specs=(P(("tensor", "dp"), None), P(("tensor", "dp"), None), P(("tensor", "dp"), None)),
        check_vma=False,
    )
```

```python
import functools

import jax
import jax.numpy as jnp
from jax import lax
from jax.experimental import pallas as pl
from jax.experimental.pallas import tpu as pltpu
from jax.sharding import PartitionSpec as P


MESH = pl.DeviceIdType.MESH


def exchange_kernel(
    ndp, nt, tok_ref, prj_ref, gate_ref, up_ref, hg_ref, out_ref,
    g_v, u_v, h_v, prj_v, cols, part, rs_buf, xp_all, grads, recv,
    load_sem, tok_send, tok_recv, rs_send, rs_recv,
    xz_send, xt_send, xc_send, xp_recv, xc_recv, g_send, g_recv,
):
    d = lax.axis_index("dp")
    t = lax.axis_index("tensor")
    nz = ndp // 2
    z, c = d // 2, d % 2
    sub = tok_ref.shape[0]
    grp = sub * nt
    dcol = tok_ref.shape[1] // nt
    rows = recv.shape[2]
    rank = prj_ref.shape[1]
    half = ndp // 2
    half_tiles = half * rows // 128

    own_half = d // half
    inner = (z * (nz - 1 - z) + nz * nz - 1) // (nz * nz)
    first = own_half * (1 - inner) + (1 - own_half) * inner

    head = -(-rows // 128)
    spans = (
        (first * half_tiles, head),
        (first * half_tiles + head, half_tiles - head),
        ((1 - first) * half_tiles, half_tiles),
    )
    loads = []
    for i, (start, count) in enumerate(spans):
        at = pl.ds(pl.multiple_of(start * 128, 128), count * 128)
        for k, (src, dst) in enumerate(((gate_ref, g_v), (up_ref, u_v), (hg_ref, h_v))):
            loads.append(
                pltpu.make_async_copy(src.at[:, at], dst.at[:, at], load_sem.at[3 * i + k])
            )
    load_prj = pltpu.make_async_copy(prj_ref, prj_v, load_sem.at[9])
    own_tok = pltpu.make_async_copy(
        tok_ref.at[:, pl.ds(pl.multiple_of(t * dcol, 128), dcol)],
        cols.at[pl.ds(pl.multiple_of(t * sub, 16), sub), :],
        load_sem.at[10],
    )
    for load in loads[:3]:
        load.start()

    barrier = pltpu.get_barrier_semaphore()
    for k in range(1, ndp):
        pl.semaphore_signal(barrier, inc=1, device_id=((d + k) % ndp, t), device_id_type=MESH)
    for k in range(1, nt):
        pl.semaphore_signal(barrier, inc=1, device_id=(d, (t + k) % nt), device_id_type=MESH)

    for load in loads[3:]:
        load.start()
    load_prj.start()
    own_tok.start()

    def tok_copy(dest, src):
        return pltpu.make_async_remote_copy(
            src_ref=tok_ref.at[:, pl.ds(pl.multiple_of(dest * dcol, 128), dcol)],
            dst_ref=cols.at[pl.ds(pl.multiple_of(src * sub, 16), sub), :],
            send_sem=tok_send.at[dest],
            recv_sem=tok_recv.at[src],
            device_id=(d, dest),
            device_id_type=MESH,
        )

    def tile(i, carry):
        at = pl.ds(pl.multiple_of(i * 128, 128), 128)
        gate = g_v[:, at].astype(jnp.float32)
        upval = u_v[:, at].astype(jnp.float32)
        hgrad = h_v[:, at].astype(jnp.float32)
        sig = jax.nn.sigmoid(gate)
        grad_gate = hgrad * upval * sig * (1.0 + gate * (1.0 - sig))
        grad_up = hgrad * gate * sig
        grads[0, at, :] = grad_gate.astype(jnp.bfloat16).T
        grads[1, at, :] = grad_up.astype(jnp.bfloat16).T
        return carry

    def block_of(dest):
        return grads.at[:, pl.ds(pl.multiple_of(dest * rows, 16), rows), :]

    def grad_copy(dest, src):
        return pltpu.make_async_remote_copy(
            src_ref=block_of(dest),
            dst_ref=recv.at[src],
            send_sem=g_send.at[dest],
            recv_sem=g_recv.at[src],
            device_id=(dest, t),
            device_id_type=MESH,
        )

    own_grad = pltpu.make_async_copy(block_of(d), recv.at[d], load_sem.at[11])

    def send_block(dest):
        @pl.when(dest != d)
        def _():
            grad_copy(dest, d).start()

        @pl.when(dest == d)
        def _():
            own_grad.start()

    def tiles_of(which, start, stop):
        lax.fori_loop(which * half_tiles + start, which * half_tiles + stop, tile, 0)

    pl.semaphore_wait(barrier, ndp + nt - 2)
    for k in range(1, nt):
        tok_copy((t + k) % nt, t).start()
    for load in loads[:3]:
        load.wait()
    tiles_of(first, 0, head)
    send_block(first * half)

    for load in loads[3:6]:
        load.wait()
    done = head
    for j in range(1, half):
        need = -(-((j + 1) * rows) // 128)
        tiles_of(first, done, need)
        done = need
        if j < 2:
            send_block(first * half + j)
        else:
            pl.when(inner == 0)(functools.partial(send_block, first * half + j))
    for load in loads[6:]:
        load.wait()
    tiles_of(1 - first, 0, half_tiles)

    load_prj.wait()
    own_tok.wait()
    for k in range(1, nt):
        tok_copy(t, (t + k) % nt).wait_recv()
    part[...] = jnp.dot(cols[...], prj_v[...], preferred_element_type=jnp.float32)

    def rs_copy(dest, src):
        return pltpu.make_async_remote_copy(
            src_ref=part.at[pl.ds(pl.multiple_of(dest * sub, 16), sub), :],
            dst_ref=rs_buf.at[src],
            send_sem=rs_send.at[dest],
            recv_sem=rs_recv.at[src],
            device_id=(d, dest),
            device_id_type=MESH,
        )

    for k in range(1, nt):
        rs_copy((t + k) % nt, t).start()
    rs_buf[t] = part[pl.ds(pl.multiple_of(t * sub, 16), sub), :]
    for k in range(1, nt):
        rs_copy(t, (t + k) % nt).wait_recv()
    total = rs_buf[0]
    for k in range(1, nt):
        total = total + rs_buf[k]

    def piece(dd, tt):
        return xp_all.at[pl.ds(pl.multiple_of(dd * grp + tt * sub, 16), sub), :]

    xp_all[pl.ds(pl.multiple_of(d * grp + t * sub, 16), sub), :] = total.astype(jnp.bfloat16)

    def piece_copy(dd, tt, send_sem, dest):
        return pltpu.make_async_remote_copy(
            src_ref=piece(dd, tt),
            dst_ref=piece(dd, tt),
            send_sem=send_sem,
            recv_sem=xp_recv.at[dd * nt + tt],
            device_id=dest,
            device_id_type=MESH,
        )

    for k in range(1, nz):
        zz = (z + k) % nz
        piece_copy(d, t, xz_send.at[zz], (zz * 2 + c, t)).start()

    for j in range(2, half):
        pl.when(inner == 1)(functools.partial(send_block, first * half + j))
    for j in range(half):
        send_block((1 - first) * half + j)

    if nz == 4:
        order = [z, z + 1 - 2 * (z % 2), 3 - 3 * (z // 2), 2 - z // 2]
    else:
        order = [(z + k) % nz for k in range(nz)]

    for k, zz in enumerate(order):
        dd = zz * 2 + c
        if k:
            piece_copy(dd, t, xz_send.at[zz], (dd, t)).wait_recv()
        for kt in range(1, nt):
            tt = (t + kt) % nt
            piece_copy(dd, t, xt_send.at[zz * nt + tt], (d, tt)).start()

    partner = d + 1 - 2 * c

    def core_copy(zz, parity):
        group = xp_all.at[pl.ds(pl.multiple_of((zz * 2 + parity) * grp, 128), grp), :]
        return pltpu.make_async_remote_copy(
            src_ref=group,
            dst_ref=group,
            send_sem=xc_send.at[zz],
            recv_sem=xc_recv.at[zz],
            device_id=(partner, t),
            device_id_type=MESH,
        )

    for zz in order:
        for kt in range(1, nt):
            tt = (t + kt) % nt
            piece_copy(zz * 2 + c, tt, xt_send.at[zz * nt + tt], (d, tt)).wait_recv()
        core_copy(zz, c).start()

    for k, zz in enumerate(order):
        core_copy(zz, 1 - c).wait_recv()
        if k == 0:
            own_grad.wait()
            grad_copy(d, partner).wait_recv()
        else:
            grad_copy(d, zz * 2).wait_recv()
            grad_copy(d, zz * 2 + 1).wait_recv()
        xp = xp_all[pl.ds(pl.multiple_of(zz * 2 * grp, 128), 2 * grp), :]
        for part_of in (0, 1):
            lhs = jnp.concatenate([recv[zz * 2, part_of], recv[zz * 2 + 1, part_of]], axis=1)
            term = jnp.dot(lhs, xp, preferred_element_type=jnp.float32)
            at = slice(part_of * rank, (part_of + 1) * rank)
            if k == 0:
                out_ref[:, at] = term
            else:
                out_ref[:, at] += term

    for k in range(1, nt):
        dest = (t + k) % nt
        tok_copy(dest, t).wait_send()
        rs_copy(dest, t).wait_send()
        for zz in range(nz):
            piece_copy(zz * 2 + c, t, xt_send.at[zz * nt + dest], (d, dest)).wait_send()
    for k in range(1, nz):
        zz = (z + k) % nz
        piece_copy(d, t, xz_send.at[zz], (zz * 2 + c, t)).wait_send()
    for zz in range(nz):
        core_copy(zz, c).wait_send()
    for k in range(1, ndp):
        grad_copy((d + k) % ndp, d).wait_send()


def exchange(ndp, nt, tokens_in, projector, gate_pre, up_pre, hidden_grad):
    sub, width = tokens_in.shape
    depth, rank = projector.shape
    grp, cols = gate_pre.shape
    rows = cols // ndp
    dma = pltpu.SemaphoreType.DMA
    bf, f32 = jnp.bfloat16, jnp.float32
    nz = ndp // 2
    operands = (tokens_in, projector, gate_pre, up_pre, hidden_grad)
    flops = 2 * grp * depth * rank + 4 * rows * grp * ndp * rank
    return pl.pallas_call(
        functools.partial(exchange_kernel, ndp, nt),
        out_shape=jax.ShapeDtypeStruct((rows, 2 * rank), f32),
        in_specs=[pl.BlockSpec(memory_space=pltpu.HBM)] * 5,
        out_specs=pl.BlockSpec(memory_space=pltpu.VMEM),
        scratch_shapes=[
            pltpu.VMEM((grp, cols), bf),
            pltpu.VMEM((grp, cols), bf),
            pltpu.VMEM((grp, cols), bf),
            pltpu.VMEM((depth, rank), bf),
            pltpu.VMEM((grp, depth), bf),
            pltpu.VMEM((grp, rank), f32),
            pltpu.VMEM((nt, sub, rank), f32),
            pltpu.VMEM((grp * ndp, rank), bf),
            pltpu.VMEM((2, cols, grp), bf),
            pltpu.VMEM((ndp, 2, rows, grp), bf),
            dma((12,)),
            dma((nt,)),
            dma((nt,)),
            dma((nt,)),
            dma((nt,)),
            dma((nz,)),
            dma((nz * nt,)),
            dma((nz,)),
            dma((ndp * nt,)),
            dma((nz,)),
            dma((ndp,)),
            dma((ndp,)),
        ],
        compiler_params=pltpu.CompilerParams(
            collective_id=0, has_side_effects=True, vmem_limit_bytes=32 * 1024 * 1024
        ),
        cost_estimate=pl.CostEstimate(
            flops=flops, bytes_accessed=8 * grp * cols, transcendentals=grp * cols
        ),
    )(*[pltpu.with_memory_space_constraint(x, pltpu.HBM) for x in operands])


def fits(ndp, nt, tokens_in, projector, gate_pre):
    sub, width = tokens_in.shape
    grp, cols = gate_pre.shape
    return (
        ndp % 2 == 0
        and ndp >= 4
        and nt >= 2
        and grp == 128
        and sub * nt == grp
        and sub % 16 == 0
        and cols % ndp == 0
        and (cols // ndp) % 16 == 0
        and cols % 256 == 0
        and width % (128 * nt) == 0
        and projector.shape[0] == width // nt
        and projector.shape[1] % 128 == 0
        and cols <= 8192
        and projector.size <= 2**21
        and grp * ndp <= 4096
    )


def finish(summed, total_tokens, moment_m, moment_v):
    proj = summed * float(total_tokens) ** (-0.5)
    m_next = 0.9 * moment_m + 0.1 * proj
    v_next = 0.95 * moment_v + 0.05 * proj * proj
    direction = m_next / (jnp.sqrt(v_next) + 1e-08)
    return (m_next, v_next, direction)


def local(tokens_in, projector, gate_pre, up_pre, hidden_grad, moment_m, moment_v):
    ndp, nt = lax.axis_size("dp"), lax.axis_size("tensor")
    if fits(ndp, nt, tokens_in, projector, gate_pre):
        summed = exchange(ndp, nt, tokens_in, projector, gate_pre, up_pre, hidden_grad)
        return finish(summed, gate_pre.shape[0] * ndp, moment_m, moment_v)
    gate = gate_pre.astype(jnp.float32)
    hgrad = hidden_grad.astype(jnp.float32)
    sig = jax.nn.sigmoid(gate)
    upval = up_pre.astype(jnp.float32)
    grad_gate = (hgrad * upval * sig * (1.0 + gate * (1.0 - sig))).astype(jnp.bfloat16)
    grad_up = (hgrad * gate * sig).astype(jnp.bfloat16)
    grads = jnp.stack([grad_gate, grad_up])
    grads = lax.all_to_all(grads, "dp", split_axis=2, concat_axis=1, tiled=True)
    columns = lax.all_to_all(tokens_in, "tensor", split_axis=1, concat_axis=0, tiled=True)
    partial_xp = jnp.dot(columns, projector, preferred_element_type=jnp.float32)
    own_rows = lax.psum_scatter(partial_xp, "tensor", scatter_dimension=0, tiled=True).astype(
        jnp.bfloat16
    )
    xp = lax.all_gather(own_rows, ("dp", "tensor"), axis=0, tiled=True)
    contract = (((0,), (0,)), ((), ()))
    halves = [
        lax.dot_general(grads[k], xp, contract, preferred_element_type=jnp.float32) for k in (0, 1)
    ]
    summed = jnp.concatenate(halves, axis=1)
    return finish(summed, xp.shape[0], moment_m, moment_v)


def solution(mesh):
    return jax.shard_map(
        local,
        mesh=mesh,
        in_specs=(
            P(("dp", "tensor"), None),
            P("tensor", None),
            P("dp", "tensor"),
            P("dp", "tensor"),
            P("dp", "tensor"),
            P(("tensor", "dp"), None),
            P(("tensor", "dp"), None),
        ),
        out_specs=(P(("tensor", "dp"), None), P(("tensor", "dp"), None), P(("tensor", "dp"), None)),
        check_vma=False,
    )
```

```python
import functools

import jax
import jax.numpy as jnp
from jax import lax
from jax.experimental import pallas as pl
from jax.experimental.pallas import tpu as pltpu
from jax.sharding import PartitionSpec as P


MESH = pl.DeviceIdType.MESH
HELD = 5


def exchange_kernel(
    ndp, nt, tok_ref, prj_ref, gate_ref, up_ref, hg_ref, out_ref,
    g_v, u_v, h_v, prj_v, cols, part, rs_buf, xp_all, grads, recv,
    load_sem, tok_send, tok_recv, rs_send, rs_recv,
    xz_send, xt_send, xc_send, xp_recv, xc_recv, g_send, g_recv,
):
    d = lax.axis_index("dp")
    t = lax.axis_index("tensor")
    nz = ndp // 2
    z, c = d // 2, d % 2
    sub = tok_ref.shape[0]
    grp = sub * nt
    dcol = tok_ref.shape[1] // nt
    rows = recv.shape[2]
    rank = prj_ref.shape[1]
    half = ndp // 2
    half_tiles = half * rows // 128

    own_half = d // half
    inner = (z * (nz - 1 - z) + nz * nz - 1) // (nz * nz)
    first = own_half * (1 - inner) + (1 - own_half) * inner

    head = -(-rows // 128)
    spans = (
        (first * half_tiles, head),
        (first * half_tiles + head, half_tiles - head),
        ((1 - first) * half_tiles, half_tiles),
    )
    loads = []
    for i, (start, count) in enumerate(spans):
        at = pl.ds(pl.multiple_of(start * 128, 128), count * 128)
        for k, (src, dst) in enumerate(((gate_ref, g_v), (up_ref, u_v), (hg_ref, h_v))):
            loads.append(
                pltpu.make_async_copy(src.at[:, at], dst.at[:, at], load_sem.at[3 * i + k])
            )
    load_prj = pltpu.make_async_copy(prj_ref, prj_v, load_sem.at[9])
    own_tok = pltpu.make_async_copy(
        tok_ref.at[:, pl.ds(pl.multiple_of(t * dcol, 128), dcol)],
        cols.at[pl.ds(pl.multiple_of(t * sub, 16), sub), :],
        load_sem.at[10],
    )
    for load in loads[:3]:
        load.start()

    barrier = pltpu.get_barrier_semaphore()
    for k in range(1, ndp):
        pl.semaphore_signal(barrier, inc=1, device_id=((d + k) % ndp, t), device_id_type=MESH)
    for k in range(1, nt):
        pl.semaphore_signal(barrier, inc=1, device_id=(d, (t + k) % nt), device_id_type=MESH)

    for load in loads[3:]:
        load.start()
    load_prj.start()
    own_tok.start()

    def tok_copy(dest, src):
        return pltpu.make_async_remote_copy(
            src_ref=tok_ref.at[:, pl.ds(pl.multiple_of(dest * dcol, 128), dcol)],
            dst_ref=cols.at[pl.ds(pl.multiple_of(src * sub, 16), sub), :],
            send_sem=tok_send.at[dest],
            recv_sem=tok_recv.at[src],
            device_id=(d, dest),
            device_id_type=MESH,
        )

    def tile(i, carry):
        at = pl.ds(pl.multiple_of(i * 128, 128), 128)
        gate = g_v[:, at].astype(jnp.float32)
        upval = u_v[:, at].astype(jnp.float32)
        hgrad = h_v[:, at].astype(jnp.float32)
        sig = jax.nn.sigmoid(gate)
        grad_gate = hgrad * upval * sig * (1.0 + gate * (1.0 - sig))
        grad_up = hgrad * gate * sig
        grads[0, at, :] = grad_gate.astype(jnp.bfloat16).T
        grads[1, at, :] = grad_up.astype(jnp.bfloat16).T
        return carry

    def block_of(dest, side):
        return grads.at[side, pl.ds(pl.multiple_of(dest * rows, 16), rows), :]

    def grad_copy(dest, src, side):
        return pltpu.make_async_remote_copy(
            src_ref=block_of(dest, side),
            dst_ref=recv.at[src, side],
            send_sem=g_send.at[2 * dest + side],
            recv_sem=g_recv.at[2 * src + side],
            device_id=(dest, t),
            device_id_type=MESH,
        )

    def own_grad(side):
        return pltpu.make_async_copy(block_of(d, side), recv.at[d, side], load_sem.at[11 + side])

    def send_block(dest, side):
        @pl.when(dest != d)
        def _():
            grad_copy(dest, d, side).start()

        @pl.when(dest == d)
        def _():
            own_grad(side).start()

    def tiles_of(which, start, stop):
        lax.fori_loop(which * half_tiles + start, which * half_tiles + stop, tile, 0)

    pl.semaphore_wait(barrier, ndp + nt - 2)
    for k in range(1, nt):
        tok_copy((t + k) % nt, t).start()
    for load in loads[:3]:
        load.wait()
    tiles_of(first, 0, head)
    for side in (0, 1):
        send_block(first * half, side)

    for load in loads[3:6]:
        load.wait()
    done = head
    for j in range(1, half):
        need = -(-((j + 1) * rows) // 128)
        tiles_of(first, done, need)
        done = need
        for side in (0, 1):
            send = functools.partial(send_block, first * half + j, side)
            if 2 * j + side < HELD:
                send()
            else:
                pl.when(inner == 0)(send)
    for load in loads[6:]:
        load.wait()
    tiles_of(1 - first, 0, half_tiles)

    load_prj.wait()
    own_tok.wait()
    for k in range(1, nt):
        tok_copy(t, (t + k) % nt).wait_recv()
    part[...] = jnp.dot(cols[...], prj_v[...], preferred_element_type=jnp.float32)

    def rs_copy(dest, src):
        return pltpu.make_async_remote_copy(
            src_ref=part.at[pl.ds(pl.multiple_of(dest * sub, 16), sub), :],
            dst_ref=rs_buf.at[src],
            send_sem=rs_send.at[dest],
            recv_sem=rs_recv.at[src],
            device_id=(d, dest),
            device_id_type=MESH,
        )

    for k in range(1, nt):
        rs_copy((t + k) % nt, t).start()
    rs_buf[t] = part[pl.ds(pl.multiple_of(t * sub, 16), sub), :]
    for k in range(1, nt):
        rs_copy(t, (t + k) % nt).wait_recv()
    total = rs_buf[0]
    for k in range(1, nt):
        total = total + rs_buf[k]

    def piece(dd, tt):
        return xp_all.at[pl.ds(pl.multiple_of(dd * grp + tt * sub, 16), sub), :]

    xp_all[pl.ds(pl.multiple_of(d * grp + t * sub, 16), sub), :] = total.astype(jnp.bfloat16)

    def piece_copy(dd, tt, send_sem, dest):
        return pltpu.make_async_remote_copy(
            src_ref=piece(dd, tt),
            dst_ref=piece(dd, tt),
            send_sem=send_sem,
            recv_sem=xp_recv.at[dd * nt + tt],
            device_id=dest,
            device_id_type=MESH,
        )

    for k in range(1, nz):
        zz = (z + k) % nz
        piece_copy(d, t, xz_send.at[zz], (zz * 2 + c, t)).start()

    for j in range(half):
        for side in (0, 1):
            if 2 * j + side >= HELD:
                send = functools.partial(send_block, first * half + j, side)
                pl.when(inner == 1)(send)
    for j in range(half):
        for side in (0, 1):
            send_block((1 - first) * half + j, side)

    if nz == 4:
        order = [z, z + 1 - 2 * (z % 2), 3 - 3 * (z // 2), 2 - z // 2]
    else:
        order = [(z + k) % nz for k in range(nz)]

    for k, zz in enumerate(order):
        dd = zz * 2 + c
        if k:
            piece_copy(dd, t, xz_send.at[zz], (dd, t)).wait_recv()
        for kt in range(1, nt):
            tt = (t + kt) % nt
            piece_copy(dd, t, xt_send.at[zz * nt + tt], (d, tt)).start()

    partner = d + 1 - 2 * c

    def core_copy(zz, parity):
        group = xp_all.at[pl.ds(pl.multiple_of((zz * 2 + parity) * grp, 128), grp), :]
        return pltpu.make_async_remote_copy(
            src_ref=group,
            dst_ref=group,
            send_sem=xc_send.at[zz],
            recv_sem=xc_recv.at[zz],
            device_id=(partner, t),
            device_id_type=MESH,
        )

    for zz in order:
        for kt in range(1, nt):
            tt = (t + kt) % nt
            piece_copy(zz * 2 + c, tt, xt_send.at[zz * nt + tt], (d, tt)).wait_recv()
        core_copy(zz, c).start()

    for k, zz in enumerate(order):
        core_copy(zz, 1 - c).wait_recv()
        xp = xp_all[pl.ds(pl.multiple_of(zz * 2 * grp, 128), 2 * grp), :]
        for part_of in (0, 1):
            if k == 0:
                own_grad(part_of).wait()
                grad_copy(d, partner, part_of).wait_recv()
            else:
                grad_copy(d, zz * 2, part_of).wait_recv()
                grad_copy(d, zz * 2 + 1, part_of).wait_recv()
            lhs = jnp.concatenate([recv[zz * 2, part_of], recv[zz * 2 + 1, part_of]], axis=1)
            term = jnp.dot(lhs, xp, preferred_element_type=jnp.float32)
            at = slice(part_of * rank, (part_of + 1) * rank)
            if k == 0:
                out_ref[:, at] = term
            else:
                out_ref[:, at] += term

    for k in range(1, nt):
        dest = (t + k) % nt
        tok_copy(dest, t).wait_send()
        rs_copy(dest, t).wait_send()
        for zz in range(nz):
            piece_copy(zz * 2 + c, t, xt_send.at[zz * nt + dest], (d, dest)).wait_send()
    for k in range(1, nz):
        zz = (z + k) % nz
        piece_copy(d, t, xz_send.at[zz], (zz * 2 + c, t)).wait_send()
    for zz in range(nz):
        core_copy(zz, c).wait_send()
    for k in range(1, ndp):
        for side in (0, 1):
            grad_copy((d + k) % ndp, d, side).wait_send()


def exchange(ndp, nt, tokens_in, projector, gate_pre, up_pre, hidden_grad):
    sub, width = tokens_in.shape
    depth, rank = projector.shape
    grp, cols = gate_pre.shape
    rows = cols // ndp
    dma = pltpu.SemaphoreType.DMA
    bf, f32 = jnp.bfloat16, jnp.float32
    nz = ndp // 2
    operands = (tokens_in, projector, gate_pre, up_pre, hidden_grad)
    flops = 2 * grp * depth * rank + 4 * rows * grp * ndp * rank
    return pl.pallas_call(
        functools.partial(exchange_kernel, ndp, nt),
        out_shape=jax.ShapeDtypeStruct((rows, 2 * rank), f32),
        in_specs=[pl.BlockSpec(memory_space=pltpu.HBM)] * 5,
        out_specs=pl.BlockSpec(memory_space=pltpu.VMEM),
        scratch_shapes=[
            pltpu.VMEM((grp, cols), bf),
            pltpu.VMEM((grp, cols), bf),
            pltpu.VMEM((grp, cols), bf),
            pltpu.VMEM((depth, rank), bf),
            pltpu.VMEM((grp, depth), bf),
            pltpu.VMEM((grp, rank), f32),
            pltpu.VMEM((nt, sub, rank), f32),
            pltpu.VMEM((grp * ndp, rank), bf),
            pltpu.VMEM((2, cols, grp), bf),
            pltpu.VMEM((ndp, 2, rows, grp), bf),
            dma((13,)),
            dma((nt,)),
            dma((nt,)),
            dma((nt,)),
            dma((nt,)),
            dma((nz,)),
            dma((nz * nt,)),
            dma((nz,)),
            dma((ndp * nt,)),
            dma((nz,)),
            dma((2 * ndp,)),
            dma((2 * ndp,)),
        ],
        compiler_params=pltpu.CompilerParams(
            collective_id=0, has_side_effects=True, vmem_limit_bytes=32 * 1024 * 1024
        ),
        cost_estimate=pl.CostEstimate(
            flops=flops, bytes_accessed=8 * grp * cols, transcendentals=grp * cols
        ),
    )(*[pltpu.with_memory_space_constraint(x, pltpu.HBM) for x in operands])


def fits(ndp, nt, tokens_in, projector, gate_pre):
    sub, width = tokens_in.shape
    grp, cols = gate_pre.shape
    return (
        ndp % 2 == 0
        and ndp >= 4
        and nt >= 2
        and grp == 128
        and sub * nt == grp
        and sub % 16 == 0
        and cols % ndp == 0
        and (cols // ndp) % 16 == 0
        and cols % 256 == 0
        and width % (128 * nt) == 0
        and projector.shape[0] == width // nt
        and projector.shape[1] % 128 == 0
        and cols <= 8192
        and projector.size <= 2**21
        and grp * ndp <= 4096
    )


def finish(summed, total_tokens, moment_m, moment_v):
    proj = summed * float(total_tokens) ** (-0.5)
    m_next = 0.9 * moment_m + 0.1 * proj
    v_next = 0.95 * moment_v + 0.05 * proj * proj
    direction = m_next / (jnp.sqrt(v_next) + 1e-08)
    return (m_next, v_next, direction)


def finish_kernel(total_tokens, steps, sum_ref, m_ref, v_ref, *refs):
    outs, bufs, sem = refs[:3], refs[3:6], refs[6]
    rows = sum_ref.shape[0] // steps
    copies = []
    for i in range(steps):
        at = slice(i * rows, (i + 1) * rows)
        values = finish(sum_ref[at, :], total_tokens, m_ref[at, :], v_ref[at, :])
        for k in range(3):
            bufs[k][at, :] = values[k]
            copy = pltpu.make_async_copy(
                bufs[k].at[at, :], outs[k].at[at, :], sem.at[3 * i + k]
            )
            copy.start()
            copies.append(copy)
    for copy in copies:
        copy.wait()


def finish_call(summed, total_tokens, moment_m, moment_v):
    steps = 6
    shape = jax.ShapeDtypeStruct(summed.shape, jnp.float32)
    return pl.pallas_call(
        functools.partial(finish_kernel, total_tokens, steps),
        out_shape=(shape,) * 3,
        in_specs=[pl.BlockSpec(memory_space=pltpu.VMEM)] * 3,
        out_specs=[pl.BlockSpec(memory_space=pltpu.HBM)] * 3,
        scratch_shapes=[pltpu.VMEM(summed.shape, jnp.float32)] * 3
        + [pltpu.SemaphoreType.DMA((3 * steps,))],
        compiler_params=pltpu.CompilerParams(vmem_limit_bytes=16 * 1024 * 1024),
    )(summed, moment_m, moment_v)


def local(tokens_in, projector, gate_pre, up_pre, hidden_grad, moment_m, moment_v):
    ndp, nt = lax.axis_size("dp"), lax.axis_size("tensor")
    if fits(ndp, nt, tokens_in, projector, gate_pre):
        summed = exchange(ndp, nt, tokens_in, projector, gate_pre, up_pre, hidden_grad)
        return tuple(finish_call(summed, gate_pre.shape[0] * ndp, moment_m, moment_v))
    gate = gate_pre.astype(jnp.float32)
    hgrad = hidden_grad.astype(jnp.float32)
    sig = jax.nn.sigmoid(gate)
    upval = up_pre.astype(jnp.float32)
    grad_gate = (hgrad * upval * sig * (1.0 + gate * (1.0 - sig))).astype(jnp.bfloat16)
    grad_up = (hgrad * gate * sig).astype(jnp.bfloat16)
    grads = jnp.stack([grad_gate, grad_up])
    grads = lax.all_to_all(grads, "dp", split_axis=2, concat_axis=1, tiled=True)
    columns = lax.all_to_all(tokens_in, "tensor", split_axis=1, concat_axis=0, tiled=True)
    partial_xp = jnp.dot(columns, projector, preferred_element_type=jnp.float32)
    own_rows = lax.psum_scatter(partial_xp, "tensor", scatter_dimension=0, tiled=True).astype(
        jnp.bfloat16
    )
    xp = lax.all_gather(own_rows, ("dp", "tensor"), axis=0, tiled=True)
    contract = (((0,), (0,)), ((), ()))
    halves = [
        lax.dot_general(grads[k], xp, contract, preferred_element_type=jnp.float32) for k in (0, 1)
    ]
    summed = jnp.concatenate(halves, axis=1)
    return finish(summed, xp.shape[0], moment_m, moment_v)


def solution(mesh):
    return jax.shard_map(
        local,
        mesh=mesh,
        in_specs=(
            P(("dp", "tensor"), None),
            P("tensor", None),
            P("dp", "tensor"),
            P("dp", "tensor"),
            P("dp", "tensor"),
            P(("tensor", "dp"), None),
            P(("tensor", "dp"), None),
        ),
        out_specs=(P(("tensor", "dp"), None), P(("tensor", "dp"), None), P(("tensor", "dp"), None)),
        check_vma=False,
    )
```

```python
import functools

import jax
import jax.numpy as jnp
from jax import lax
from jax.experimental import pallas as pl
from jax.experimental.pallas import tpu as pltpu
from jax.sharding import PartitionSpec as P


MESH = pl.DeviceIdType.MESH
HELD = 5


def exchange_kernel(
    ndp, nt, tok_ref, prj_ref, gate_ref, up_ref, hg_ref, out_ref,
    g_v, u_v, h_v, prj_v, cols, part, rs_buf, xp_all, grads, recv,
    load_sem, tok_send, tok_recv, rs_send, rs_recv,
    xz_send, xt_send, xc_send, xp_recv, xc_recv, g_send, g_recv,
):
    d = lax.axis_index("dp")
    t = lax.axis_index("tensor")
    nz = ndp // 2
    z, c = d // 2, d % 2
    sub = tok_ref.shape[0]
    grp = sub * nt
    dcol = tok_ref.shape[1] // nt
    rows = recv.shape[2]
    rank = prj_ref.shape[1]
    half = ndp // 2
    half_tiles = half * rows // 128

    own_half = d // half
    inner = (z * (nz - 1 - z) + nz * nz - 1) // (nz * nz)
    first = own_half * (1 - inner) + (1 - own_half) * inner

    head = -(-rows // 128)
    spans = (
        (first * half_tiles, head),
        (first * half_tiles + head, half_tiles - head),
        ((1 - first) * half_tiles, half_tiles),
    )
    loads = []
    for i, (start, count) in enumerate(spans):
        at = pl.ds(pl.multiple_of(start * 128, 128), count * 128)
        for k, (src, dst) in enumerate(((gate_ref, g_v), (up_ref, u_v), (hg_ref, h_v))):
            loads.append(
                pltpu.make_async_copy(src.at[:, at], dst.at[:, at], load_sem.at[3 * i + k])
            )
    load_prj = pltpu.make_async_copy(prj_ref, prj_v, load_sem.at[9])
    own_tok = pltpu.make_async_copy(
        tok_ref.at[:, pl.ds(pl.multiple_of(t * dcol, 128), dcol)],
        cols.at[pl.ds(pl.multiple_of(t * sub, 16), sub), :],
        load_sem.at[10],
    )
    for load in loads[:3]:
        load.start()

    barrier = pltpu.get_barrier_semaphore()
    for k in range(1, ndp):
        pl.semaphore_signal(barrier, inc=1, device_id=((d + k) % ndp, t), device_id_type=MESH)
    for k in range(1, nt):
        pl.semaphore_signal(barrier, inc=1, device_id=(d, (t + k) % nt), device_id_type=MESH)

    for load in loads[3:]:
        load.start()
    load_prj.start()
    own_tok.start()

    def tok_copy(dest, src):
        return pltpu.make_async_remote_copy(
            src_ref=tok_ref.at[:, pl.ds(pl.multiple_of(dest * dcol, 128), dcol)],
            dst_ref=cols.at[pl.ds(pl.multiple_of(src * sub, 16), sub), :],
            send_sem=tok_send.at[dest],
            recv_sem=tok_recv.at[src],
            device_id=(d, dest),
            device_id_type=MESH,
        )

    def tile(i, carry):
        at = pl.ds(pl.multiple_of(i * 128, 128), 128)
        gate = g_v[:, at].astype(jnp.float32)
        upval = u_v[:, at].astype(jnp.float32)
        hgrad = h_v[:, at].astype(jnp.float32)
        sig = jax.nn.sigmoid(gate)
        grad_gate = hgrad * upval * sig * (1.0 + gate * (1.0 - sig))
        grad_up = hgrad * gate * sig
        grads[0, at, :] = grad_gate.astype(jnp.bfloat16).T
        grads[1, at, :] = grad_up.astype(jnp.bfloat16).T
        return carry

    def block_of(dest, side):
        return grads.at[side, pl.ds(pl.multiple_of(dest * rows, 16), rows), :]

    def grad_copy(dest, src, side):
        return pltpu.make_async_remote_copy(
            src_ref=block_of(dest, side),
            dst_ref=recv.at[src, side],
            send_sem=g_send.at[2 * dest + side],
            recv_sem=g_recv.at[2 * src + side],
            device_id=(dest, t),
            device_id_type=MESH,
        )

    def own_grad(side):
        return pltpu.make_async_copy(block_of(d, side), recv.at[d, side], load_sem.at[11 + side])

    def send_block(dest, side):
        @pl.when(dest != d)
        def _():
            grad_copy(dest, d, side).start()

        @pl.when(dest == d)
        def _():
            own_grad(side).start()

    def tiles_of(which, start, stop):
        lax.fori_loop(which * half_tiles + start, which * half_tiles + stop, tile, 0)

    for load in loads[:3]:
        load.wait()
    tiles_of(first, 0, head)
    pl.semaphore_wait(barrier, ndp + nt - 2)
    for k in range(1, nt):
        tok_copy((t + k) % nt, t).start()
    for side in (0, 1):
        send_block(first * half, side)

    for load in loads[3:6]:
        load.wait()
    done = head
    for j in range(1, half):
        need = -(-((j + 1) * rows) // 128)
        tiles_of(first, done, need)
        done = need
        for side in (0, 1):
            send = functools.partial(send_block, first * half + j, side)
            if 2 * j + side < HELD:
                send()
            else:
                pl.when(inner == 0)(send)
    for load in loads[6:]:
        load.wait()
    tiles_of(1 - first, 0, half_tiles)

    load_prj.wait()
    own_tok.wait()
    for k in range(1, nt):
        tok_copy(t, (t + k) % nt).wait_recv()
    part[...] = jnp.dot(cols[...], prj_v[...], preferred_element_type=jnp.float32)

    def rs_copy(dest, src):
        return pltpu.make_async_remote_copy(
            src_ref=part.at[pl.ds(pl.multiple_of(dest * sub, 16), sub), :],
            dst_ref=rs_buf.at[src],
            send_sem=rs_send.at[dest],
            recv_sem=rs_recv.at[src],
            device_id=(d, dest),
            device_id_type=MESH,
        )

    for k in range(1, nt):
        rs_copy((t + k) % nt, t).start()
    rs_buf[t] = part[pl.ds(pl.multiple_of(t * sub, 16), sub), :]
    for k in range(1, nt):
        rs_copy(t, (t + k) % nt).wait_recv()
    total = rs_buf[0]
    for k in range(1, nt):
        total = total + rs_buf[k]

    def piece(dd, tt):
        return xp_all.at[pl.ds(pl.multiple_of(dd * grp + tt * sub, 16), sub), :]

    xp_all[pl.ds(pl.multiple_of(d * grp + t * sub, 16), sub), :] = total.astype(jnp.bfloat16)

    def piece_copy(dd, tt, send_sem, dest):
        return pltpu.make_async_remote_copy(
            src_ref=piece(dd, tt),
            dst_ref=piece(dd, tt),
            send_sem=send_sem,
            recv_sem=xp_recv.at[dd * nt + tt],
            device_id=dest,
            device_id_type=MESH,
        )

    for k in range(1, nz):
        zz = (z + k) % nz
        piece_copy(d, t, xz_send.at[zz], (zz * 2 + c, t)).start()

    for j in range(half):
        for side in (0, 1):
            if 2 * j + side >= HELD:
                send = functools.partial(send_block, first * half + j, side)
                pl.when(inner == 1)(send)
    for j in range(half):
        for side in (0, 1):
            send_block((1 - first) * half + j, side)

    if nz == 4:
        order = [z, z + 1 - 2 * (z % 2), 3 - 3 * (z // 2), 2 - z // 2]
    else:
        order = [(z + k) % nz for k in range(nz)]

    for k, zz in enumerate(order):
        dd = zz * 2 + c
        if k:
            piece_copy(dd, t, xz_send.at[zz], (dd, t)).wait_recv()
        for kt in range(1, nt):
            tt = (t + kt) % nt
            piece_copy(dd, t, xt_send.at[zz * nt + tt], (d, tt)).start()

    partner = d + 1 - 2 * c

    def core_copy(zz, parity):
        group = xp_all.at[pl.ds(pl.multiple_of((zz * 2 + parity) * grp, 128), grp), :]
        return pltpu.make_async_remote_copy(
            src_ref=group,
            dst_ref=group,
            send_sem=xc_send.at[zz],
            recv_sem=xc_recv.at[zz],
            device_id=(partner, t),
            device_id_type=MESH,
        )

    for zz in order:
        for kt in range(1, nt):
            tt = (t + kt) % nt
            piece_copy(zz * 2 + c, tt, xt_send.at[zz * nt + tt], (d, tt)).wait_recv()
        core_copy(zz, c).start()

    for k, zz in enumerate(order):
        core_copy(zz, 1 - c).wait_recv()
        xp = xp_all[pl.ds(pl.multiple_of(zz * 2 * grp, 128), 2 * grp), :]
        for part_of in (0, 1):
            if k == 0:
                own_grad(part_of).wait()
                grad_copy(d, partner, part_of).wait_recv()
            else:
                grad_copy(d, zz * 2, part_of).wait_recv()
                grad_copy(d, zz * 2 + 1, part_of).wait_recv()
            lhs = jnp.concatenate([recv[zz * 2, part_of], recv[zz * 2 + 1, part_of]], axis=1)
            term = jnp.dot(lhs, xp, preferred_element_type=jnp.float32)
            at = slice(part_of * rank, (part_of + 1) * rank)
            if k == 0:
                out_ref[:, at] = term
            else:
                out_ref[:, at] += term

    for k in range(1, nt):
        dest = (t + k) % nt
        tok_copy(dest, t).wait_send()
        rs_copy(dest, t).wait_send()
        for zz in range(nz):
            piece_copy(zz * 2 + c, t, xt_send.at[zz * nt + dest], (d, dest)).wait_send()
    for k in range(1, nz):
        zz = (z + k) % nz
        piece_copy(d, t, xz_send.at[zz], (zz * 2 + c, t)).wait_send()
    for zz in range(nz):
        core_copy(zz, c).wait_send()
    for k in range(1, ndp):
        for side in (0, 1):
            grad_copy((d + k) % ndp, d, side).wait_send()


def exchange(ndp, nt, tokens_in, projector, gate_pre, up_pre, hidden_grad):
    sub, width = tokens_in.shape
    depth, rank = projector.shape
    grp, cols = gate_pre.shape
    rows = cols // ndp
    dma = pltpu.SemaphoreType.DMA
    bf, f32 = jnp.bfloat16, jnp.float32
    nz = ndp // 2
    operands = (tokens_in, projector, gate_pre, up_pre, hidden_grad)
    flops = 2 * grp * depth * rank + 4 * rows * grp * ndp * rank
    return pl.pallas_call(
        functools.partial(exchange_kernel, ndp, nt),
        out_shape=jax.ShapeDtypeStruct((rows, 2 * rank), f32),
        in_specs=[pl.BlockSpec(memory_space=pltpu.HBM)] * 5,
        out_specs=pl.BlockSpec(memory_space=pltpu.VMEM),
        scratch_shapes=[
            pltpu.VMEM((grp, cols), bf),
            pltpu.VMEM((grp, cols), bf),
            pltpu.VMEM((grp, cols), bf),
            pltpu.VMEM((depth, rank), bf),
            pltpu.VMEM((grp, depth), bf),
            pltpu.VMEM((grp, rank), f32),
            pltpu.VMEM((nt, sub, rank), f32),
            pltpu.VMEM((grp * ndp, rank), bf),
            pltpu.VMEM((2, cols, grp), bf),
            pltpu.VMEM((ndp, 2, rows, grp), bf),
            dma((13,)),
            dma((nt,)),
            dma((nt,)),
            dma((nt,)),
            dma((nt,)),
            dma((nz,)),
            dma((nz * nt,)),
            dma((nz,)),
            dma((ndp * nt,)),
            dma((nz,)),
            dma((2 * ndp,)),
            dma((2 * ndp,)),
        ],
        compiler_params=pltpu.CompilerParams(
            collective_id=0, has_side_effects=True, vmem_limit_bytes=32 * 1024 * 1024
        ),
        cost_estimate=pl.CostEstimate(
            flops=flops, bytes_accessed=8 * grp * cols, transcendentals=grp * cols
        ),
    )(*[pltpu.with_memory_space_constraint(x, pltpu.HBM) for x in operands])


def fits(ndp, nt, tokens_in, projector, gate_pre):
    sub, width = tokens_in.shape
    grp, cols = gate_pre.shape
    return (
        ndp % 2 == 0
        and ndp >= 4
        and nt >= 2
        and grp == 128
        and sub * nt == grp
        and sub % 16 == 0
        and cols % ndp == 0
        and (cols // ndp) % 16 == 0
        and cols % 256 == 0
        and width % (128 * nt) == 0
        and projector.shape[0] == width // nt
        and projector.shape[1] % 128 == 0
        and cols <= 8192
        and projector.size <= 2**21
        and grp * ndp <= 4096
    )


def finish(summed, total_tokens, moment_m, moment_v):
    proj = summed * float(total_tokens) ** (-0.5)
    m_next = 0.9 * moment_m + 0.1 * proj
    v_next = 0.95 * moment_v + 0.05 * proj * proj
    direction = m_next / (jnp.sqrt(v_next) + 1e-08)
    return (m_next, v_next, direction)


def finish_kernel(total_tokens, steps, sum_ref, m_ref, v_ref, *refs):
    outs, bufs, sem = refs[:3], refs[3:6], refs[6]
    rows = sum_ref.shape[0] // steps
    copies = []
    for i in range(steps):
        at = slice(i * rows, (i + 1) * rows)
        values = finish(sum_ref[at, :], total_tokens, m_ref[at, :], v_ref[at, :])
        for k in range(3):
            bufs[k][at, :] = values[k]
            copy = pltpu.make_async_copy(
                bufs[k].at[at, :], outs[k].at[at, :], sem.at[3 * i + k]
            )
            copy.start()
            copies.append(copy)
    for copy in copies:
        copy.wait()


def finish_call(summed, total_tokens, moment_m, moment_v):
    steps = 6
    shape = jax.ShapeDtypeStruct(summed.shape, jnp.float32)
    return pl.pallas_call(
        functools.partial(finish_kernel, total_tokens, steps),
        out_shape=(shape,) * 3,
        in_specs=[pl.BlockSpec(memory_space=pltpu.VMEM)] * 3,
        out_specs=[pl.BlockSpec(memory_space=pltpu.HBM)] * 3,
        scratch_shapes=[pltpu.VMEM(summed.shape, jnp.float32)] * 3
        + [pltpu.SemaphoreType.DMA((3 * steps,))],
        compiler_params=pltpu.CompilerParams(vmem_limit_bytes=16 * 1024 * 1024),
    )(summed, moment_m, moment_v)


def local(tokens_in, projector, gate_pre, up_pre, hidden_grad, moment_m, moment_v):
    ndp, nt = lax.axis_size("dp"), lax.axis_size("tensor")
    if fits(ndp, nt, tokens_in, projector, gate_pre):
        summed = exchange(ndp, nt, tokens_in, projector, gate_pre, up_pre, hidden_grad)
        return tuple(finish_call(summed, gate_pre.shape[0] * ndp, moment_m, moment_v))
    gate = gate_pre.astype(jnp.float32)
    hgrad = hidden_grad.astype(jnp.float32)
    sig = jax.nn.sigmoid(gate)
    upval = up_pre.astype(jnp.float32)
    grad_gate = (hgrad * upval * sig * (1.0 + gate * (1.0 - sig))).astype(jnp.bfloat16)
    grad_up = (hgrad * gate * sig).astype(jnp.bfloat16)
    grads = jnp.stack([grad_gate, grad_up])
    grads = lax.all_to_all(grads, "dp", split_axis=2, concat_axis=1, tiled=True)
    columns = lax.all_to_all(tokens_in, "tensor", split_axis=1, concat_axis=0, tiled=True)
    partial_xp = jnp.dot(columns, projector, preferred_element_type=jnp.float32)
    own_rows = lax.psum_scatter(partial_xp, "tensor", scatter_dimension=0, tiled=True).astype(
        jnp.bfloat16
    )
    xp = lax.all_gather(own_rows, ("dp", "tensor"), axis=0, tiled=True)
    contract = (((0,), (0,)), ((), ()))
    halves = [
        lax.dot_general(grads[k], xp, contract, preferred_element_type=jnp.float32) for k in (0, 1)
    ]
    summed = jnp.concatenate(halves, axis=1)
    return finish(summed, xp.shape[0], moment_m, moment_v)


def solution(mesh):
    return jax.shard_map(
        local,
        mesh=mesh,
        in_specs=(
            P(("dp", "tensor"), None),
            P("tensor", None),
            P("dp", "tensor"),
            P("dp", "tensor"),
            P("dp", "tensor"),
            P(("tensor", "dp"), None),
            P(("tensor", "dp"), None),
        ),
        out_specs=(P(("tensor", "dp"), None), P(("tensor", "dp"), None), P(("tensor", "dp"), None)),
        check_vma=False,
    )
```
